32 devices in a mesh: section: 2 (over core), expert: 16 (over z, y, x).
Axes of the slice: x: 2, y: 2, z: 4, core: 2. Of those that a mesh axis runs over, the one named last changes fastest.
Arguments:
- tokens: bfloat16 [2, 2048, 2048], P('section', 'expert'), may hold values from -6 to 6
- cotangent: bfloat16 [2, 2048, 2048], P('section', 'expert'), may hold values from -3 to 3
- routes: int32 [2, 2048, 8], P('section', 'expert'), may hold values from 0 to 15, all different within a row; in each aligned block of 128 rows (0 to 127, 128 to 255, ..., all dimensions but the last counted through in order) at most 72 rows name the same one
- route_weights: bfloat16 [2, 2048, 8], P('section', 'expert'), may hold values from 0.099609375 to 1
- weights: bfloat16 [3, 16, 2048, 384], P(None, 'expert'), may hold values from -0.125 to 0.125
Outputs:
- token_grads: bfloat16 [2, 2048, 2048], P('section', 'expert')
- gate_grads: bfloat16 [2, 2048, 8], P('section', 'expert')
- weight_grads: float32 [3, 16, 2048, 384], P(None, 'expert', 'section')
The draws below stay inside these ranges and needn't reach their ends.
Inputs may be any that keep to these rules, and one draw needn't show every extreme that they name: `routes`: the 8 experts of a token differ. Among the 128 tokens of one device no expert is named more than 72 times, a bound that some block reaches.
All inputs are finite; a program needn't handle non-finite values.
Results may differ from the reference program's by a relative error of at most 0.0085.
Values may be sent and summed in bfloat16 or wider, within the bound.
A program may use at most 128 MiB of HBM per device.

```python
import math
import jax
import jax.numpy as jnp
import numpy as np
from jax import lax

D = 2048
FF = 384
TOP_K = 8
TOK_DEV = 128
EXPERTS = 16
CAP = 72
TOKENS = 2048
N_SECTION = 2
N_EXPERT = 16


def steps_of(stream_key, shape, split, least, high):
    gain = 1.0
    for dim, parts in split:
        heights = jax.random.uniform(jax.random.fold_in(jax.random.fold_in(stream_key, 6), dim), (parts,), jnp.float32, least / len(split), high / len(split))
        gain = gain * jnp.repeat(jnp.exp(heights), shape[dim] // parts).reshape((-1,) + (1,) * (len(shape) - 1 - dim))
    return gain


def assign_block(stream_key, own, number, rows, count, top, reach, lean):
    sequence = jax.random.permutation(stream_key, count)
    crowded, ordinary = load_shares(count, rows * top, reach, lean, True), load_shares(count, rows * top, reach, lean, False)
    places = jnp.arange(count)

    def named(lengths, offset_by):
        used = int((lengths > 0).sum())
        fixed = max(1, used // 4)
        moved = fixed + (places - fixed + offset_by * (used - fixed)) % max(1, count - fixed)
        return jnp.zeros((count,), jnp.int32).at[sequence[jnp.where(places < fixed, places, moved)]].set(jnp.asarray(lengths, jnp.int32))

    lengths = jnp.where(number % 4 == 0, named(crowded, number // 4), named(ordinary, number - number // 4 - 1))
    mixed = jax.random.permutation(jax.random.fold_in(own, 3), count)
    donor, sink = mixed[0:count // 2 * 2:2], mixed[1:count // 2 * 2:2]
    margin = jnp.minimum(lengths[donor] - 1, reach - lengths[sink]) // 2
    margin = jnp.where((donor == sequence[0]) | (sink == sequence[0]) | (lengths[sink] == 0), 0, jnp.maximum(margin, 0))
    moved = jax.random.randint(jax.random.fold_in(own, 4), (count // 2,), 0, 1 << 20) % (margin + 1)
    lengths = lengths.at[donor].add(-moved).at[sink].add(moved)
    labels = jnp.searchsorted(jnp.cumsum(lengths), jnp.arange(rows * top), side="right").astype(jnp.int32)
    grid = labels.reshape(top, rows).T
    grid = grid[jax.random.permutation(jax.random.fold_in(own, 1), rows)]
    offset_by = jax.random.randint(jax.random.fold_in(own, 2), (rows, 1), 0, top)
    return jnp.take_along_axis(grid, (jnp.arange(top)[None, :] + offset_by) % top, axis=1)


def load_shares(number_of, total, reach, lean, full):
    portions = [(1 << 20) // math.isqrt(standing ** lean) + 1 for standing in range(1, number_of + 1)]
    largest = reach if full else min(reach, max(-(-total // number_of), total * portions[0] // sum(portions)))
    least = 1 if total - largest >= number_of - 1 else 0
    given, rest = [largest] + [least] * (number_of - 1), total - largest - least * (number_of - 1)
    while rest > 0:
        candidates = [i for i in range(1, number_of) if given[i] < largest] or [i for i in range(1, number_of) if given[i] < reach]
        pool, remaining = sum([portions[i] for i in candidates]), rest
        for i in candidates:
            more = min(reach - given[i], max(1, remaining * portions[i] // pool), rest)
            given[i] = given[i] + more
            rest = rest - more
    return np.array(given)


def bell_draw(rng, dims, scale, most, cuts=(), kind=jnp.bfloat16):
    entries = jax.random.normal(rng, dims, jnp.float32) * scale
    if len(cuts) > 0:
        entries = steps_of(rng, dims, cuts, -0.22, 0.18) * entries
    return jnp.clip(entries, min=-most, max=most).astype(kind)


def setup_inputs(seed: int = 0) -> dict:
    arg_keys = jax.random.split(jax.random.key(seed), 6)
    tokens = bell_draw(arg_keys[0], (N_SECTION, TOKENS, D), 1.0, 6.0, ((0, 2), (1, 16)))
    cotangent = bell_draw(arg_keys[1], (N_SECTION, TOKENS, D), 0.5, 3.0, ((0, 2), (1, 16)))
    routes_keys = jax.random.split(jax.random.fold_in(arg_keys[2], 1), N_SECTION * TOKENS // TOK_DEV)
    routes_turns = jax.random.permutation(jax.random.fold_in(arg_keys[2], 3), N_SECTION * TOKENS // TOK_DEV)
    routes = jax.vmap(lambda own, number: assign_block(jax.random.fold_in(arg_keys[2], 2), own, number, TOK_DEV, EXPERTS, TOP_K, CAP, 1))(routes_keys, routes_turns).reshape((N_SECTION, TOKENS, TOP_K))
    route_weights = jnp.clip(jnp.exp(math.log(1.0) - 2.306499 * jax.random.uniform(arg_keys[3], (N_SECTION, TOKENS, TOP_K), jnp.float32) ** steps_of(arg_keys[3], (N_SECTION, TOKENS, TOP_K), ((0, 2), (1, 16)), -0.2, 0.2)), 0.099609375, 1.0).astype(jnp.bfloat16)
    weights = bell_draw(arg_keys[4], (3, EXPERTS, D, FF), D ** -0.5, 0.125, ((1, 16),))
    return {"tokens": tokens, "cotangent": cotangent, "routes": routes, "route_weights": route_weights, "weights": weights}


def slot_assign(route_block, experts, capacity):
    flat_ids = route_block.reshape(-1)
    pair_count = flat_ids.shape[0]
    one_hot = (flat_ids[:, None] == jnp.arange(experts, dtype=jnp.int32)[None, :]).astype(jnp.int32)
    before = jnp.cumsum(one_hot, axis=0) - one_hot
    slot_of = jnp.sum(before * one_hot, axis=1).astype(jnp.int32)
    slot_table = jnp.full((experts, capacity), pair_count, jnp.int32)
    slot_table = slot_table.at[flat_ids, slot_of].set(jnp.arange(pair_count, dtype=jnp.int32))
    return slot_of.reshape(route_block.shape), slot_table


def expert_step(in_rows, cot_rows, weight_rows, expert_w):
    gate_pre = jnp.dot(in_rows, expert_w[0], preferred_element_type=jnp.float32)
    up_pre = jnp.dot(in_rows, expert_w[1], preferred_element_type=jnp.float32)
    sigmoid_v = jax.nn.sigmoid(gate_pre)
    silu_v = gate_pre * sigmoid_v
    hidden = (silu_v * up_pre).astype(jnp.bfloat16)
    back_proj = jnp.dot(cot_rows, expert_w[2], preferred_element_type=jnp.float32)
    row_gate = jnp.sum(hidden.astype(jnp.float32) * back_proj, axis=1).astype(jnp.bfloat16)
    weight = weight_rows.astype(jnp.float32)[:, None]
    d_hidden = weight * back_proj
    d_gate_pre = (d_hidden * up_pre * sigmoid_v * (1.0 + gate_pre * (1.0 - sigmoid_v))).astype(jnp.bfloat16)
    d_up_pre = (d_hidden * silu_v).astype(jnp.bfloat16)
    scaled = (weight * cot_rows.astype(jnp.float32)).astype(jnp.bfloat16)
    contract_rows = (((0,), (0,)), ((), ()))
    weight_part = jnp.stack([
        lax.dot_general(in_rows, d_gate_pre, contract_rows, preferred_element_type=jnp.float32),
        lax.dot_general(in_rows, d_up_pre, contract_rows, preferred_element_type=jnp.float32),
        lax.dot_general(scaled, hidden, contract_rows, preferred_element_type=jnp.float32)])
    contract_ff = (((1,), (1,)), ((), ()))
    row_grads = (lax.dot_general(d_gate_pre, expert_w[0], contract_ff, preferred_element_type=jnp.float32)
                 + lax.dot_general(d_up_pre, expert_w[1], contract_ff, preferred_element_type=jnp.float32)).astype(jnp.bfloat16)
    return row_gate, row_grads, weight_part


def reference(tokens, cotangent, routes, route_weights, weights):
    blocks = N_EXPERT
    route_blocks = routes.reshape(N_SECTION, blocks, TOK_DEV, TOP_K)
    slots, tables = jax.vmap(jax.vmap(lambda route_block: slot_assign(route_block, EXPERTS, CAP)))(route_blocks)
    zero_row = jnp.zeros((N_SECTION, blocks, 1, D), tokens.dtype)
    tok_pad = jnp.concatenate([tokens.reshape(N_SECTION, blocks, TOK_DEV, D), zero_row], axis=2)
    cot_pad = jnp.concatenate([cotangent.reshape(N_SECTION, blocks, TOK_DEV, D), zero_row.astype(cotangent.dtype)], axis=2)
    gate_pad = jnp.concatenate([route_weights.reshape(N_SECTION, blocks, TOK_DEV * TOP_K),
                                jnp.zeros((N_SECTION, blocks, 1), route_weights.dtype)], axis=2)
    section_ix = jnp.arange(N_SECTION, dtype=jnp.int32)[:, None, None]
    block_ix = jnp.arange(blocks, dtype=jnp.int32)[None, :, None]

    def per_expert(expert):
        slot_table = tables[:, :, expert, :]
        token_ix = slot_table // TOP_K
        rows_all = tok_pad[section_ix, block_ix, token_ix]
        cots_all = cot_pad[section_ix, block_ix, token_ix]
        gate_vals = gate_pad[section_ix, block_ix, slot_table]
        expert_w = weights[:, expert]
        accum = jnp.zeros((3, D, FF), jnp.float32)
        gate_list = []
        row_list = []
        for section_no in range(N_SECTION):
            row_gate, row_grads, weight_part = expert_step(
                rows_all[section_no].reshape(-1, D), cots_all[section_no].reshape(-1, D),
                gate_vals[section_no].reshape(-1), expert_w)
            rounded = lax.optimization_barrier(weight_part.astype(jnp.bfloat16))
            accum = accum + rounded.astype(jnp.float32)
            gate_list.append(row_gate.reshape(blocks, CAP))
            row_list.append(row_grads.reshape(blocks, CAP, D))
        return jnp.stack(gate_list), jnp.stack(row_list), accum / N_SECTION

    gate_back, row_back, grads_all = lax.map(per_expert, jnp.arange(EXPERTS, dtype=jnp.int32))
    section_four = jnp.arange(N_SECTION, dtype=jnp.int32)[:, None, None]
    block_four = jnp.arange(blocks, dtype=jnp.int32)[None, :, None]
    accum = jnp.zeros((N_SECTION, blocks, TOK_DEV, D), jnp.float32)
    for position in range(TOP_K):
        accum = accum + row_back[route_blocks[..., position], section_four, block_four, slots[..., position]].astype(jnp.float32)
    token_grads = accum.astype(jnp.bfloat16).reshape(N_SECTION, TOKENS, D)
    section_five = jnp.arange(N_SECTION, dtype=jnp.int32)[:, None, None, None]
    block_five = jnp.arange(blocks, dtype=jnp.int32)[None, :, None, None]
    gate_grads = gate_back[route_blocks, section_five, block_five, slots].reshape(N_SECTION, TOKENS, TOP_K)
    weight_grads = jnp.transpose(grads_all, (1, 0, 2, 3))
    return token_grads, gate_grads, weight_grads
```

```python
import functools

import jax
import jax.numpy as jnp
from jax import lax
from jax.experimental import pallas as pl
from jax.experimental.pallas import tpu as pltpu
from jax.sharding import PartitionSpec as P

MESH = pl.DeviceIdType.MESH
LANES = 128
ROW_TILE = 16


def slot_assign(route_block, experts, capacity):
    flat_ids = route_block.reshape(-1)
    pair_count = flat_ids.shape[0]
    one_hot = (flat_ids[:, None] == jnp.arange(experts, dtype=jnp.int32)[None, :]).astype(jnp.int32)
    before = jnp.cumsum(one_hot, axis=0) - one_hot
    slot_of = jnp.sum(before * one_hot, axis=1)
    slot_table = jnp.full((experts, capacity), pair_count, jnp.int32)
    slot_table = slot_table.at[flat_ids, slot_of].set(jnp.arange(pair_count, dtype=jnp.int32))
    return (slot_of.reshape(route_block.shape), slot_table)


def expert_math(in_rows, cot_rows, weight, expert_w):
    f32 = jnp.float32
    gate_pre = jnp.dot(in_rows, expert_w[0], preferred_element_type=f32)
    up_pre = jnp.dot(in_rows, expert_w[1], preferred_element_type=f32)
    sigmoid_v = jax.nn.sigmoid(gate_pre)
    silu_v = gate_pre * sigmoid_v
    hidden = (silu_v * up_pre).astype(jnp.bfloat16)
    back_proj = jnp.dot(cot_rows, expert_w[2], preferred_element_type=f32)
    row_gate = jnp.sum(hidden.astype(f32) * back_proj, axis=1).astype(jnp.bfloat16)
    weight = weight.astype(f32)[:, None]
    d_hidden = weight * back_proj
    d_gate_pre = (d_hidden * up_pre * sigmoid_v * (1.0 + gate_pre * (1.0 - sigmoid_v))).astype(
        jnp.bfloat16
    )
    d_up_pre = (d_hidden * silu_v).astype(jnp.bfloat16)
    scaled = (weight * cot_rows.astype(f32)).astype(jnp.bfloat16)
    rows = (((0,), (0,)), ((), ()))
    weight_part = jnp.stack(
        [
            lax.dot_general(in_rows, d_gate_pre, rows, preferred_element_type=f32),
            lax.dot_general(in_rows, d_up_pre, rows, preferred_element_type=f32),
            lax.dot_general(scaled, hidden, rows, preferred_element_type=f32),
        ]
    )
    ff = (((1,), (1,)), ((), ()))
    row_grads = (
        lax.dot_general(d_gate_pre, expert_w[0], ff, preferred_element_type=f32)
        + lax.dot_general(d_up_pre, expert_w[1], ff, preferred_element_type=f32)
    ).astype(jnp.bfloat16)
    return (row_gate, row_grads, weight_part)


def section_mean(weight_part):
    partial_sum = weight_part[:, None].astype(jnp.bfloat16)
    sections = lax.axis_size("section")
    share = lax.psum_scatter(partial_sum, "section", scatter_dimension=2, tiled=True)
    return share.astype(jnp.float32) / sections


def line_order(count):
    order, low, high = [], 0, count - 1
    while low <= high:
        order.append(high)
        if low < high:
            order.append(low)
        low, high = low + 1, high - 1
    return order


def pick(table, index):
    value = table[0]
    for place in range(1, len(table)):
        value = jnp.where(index == place, table[place], value)
    return value


def fused_kernel(
    experts, split, cuts, x_hbm, c_hbm, w_hbm, weights_hbm,
    tok_out, gate_out, grad_out,
    xc, part_g, wgu, wdn, dgu, whid, sib_send, sib_recv, pair_send, pair_recv, wacc,
    rz_a, rz_b, rp_a, rp_b,
    loc_sem, bs_sem, br_sem, xs_sem, xr_sem, ls_sem, lr_sem, zs_sem, zr_sem, ps_sem, pr_sem,
    ss_sem, sr_sem, ws_sem, wr_sem, out_sem,
):
    f32, bf16 = jnp.float32, jnp.bfloat16
    z_count = experts // 4
    tok, depth = x_hbm.shape
    ff = weights_hbm.shape[2]
    sections = lax.axis_size("section")
    share = depth // sections
    sec = lax.axis_index("section")
    me = lax.axis_index("expert")
    z, yb, xb = me // 4, (me // 2) % 2, me % 2
    partner = me + 1 - 2 * xb
    peers = {
        "up": {"expert": me + 4},
        "down": {"expert": me - 4},
        "y": {"expert": me + 2 - 4 * yb},
        "x": {"expert": partner},
        "sec": {"section": 1 - sec},
    }
    has = {"up": z < z_count - 1, "down": z > 0, "y": None, "x": None, "sec": None}
    dirs = {"up": 0, "down": 1, "y": 2}
    order_z = line_order(z_count)
    early, late = range(len(cuts) - 1), len(cuts) - 1

    def when(*conds):
        conds = [cond for cond in conds if cond is not None]
        if not conds:
            return lambda body: body()
        joined = conds[0]
        for cond in conds[1:]:
            joined = joined & cond
        return pl.when(joined)

    def slot_of(fp, zz):
        return 2 * zz + (yb + fp) % 2

    own = slot_of(0, z)
    local = [
        pltpu.make_async_copy(x_hbm, xc.at[own, :, pl.ds(0, depth)], loc_sem.at[0]),
        pltpu.make_async_copy(c_hbm, xc.at[own, :, pl.ds(depth, depth)], loc_sem.at[1]),
        pltpu.make_async_copy(w_hbm, xc.at[own, :, pl.ds(2 * depth, LANES)], loc_sem.at[2]),
        pltpu.make_async_copy(weights_hbm.at[0], wgu.at[:, pl.ds(0, ff)], loc_sem.at[3]),
        pltpu.make_async_copy(weights_hbm.at[1], wgu.at[:, pl.ds(ff, ff)], loc_sem.at[4]),
        pltpu.make_async_copy(weights_hbm.at[2], wdn.at[:, pl.ds(0, ff)], loc_sem.at[5]),
    ]
    for copy in local:
        copy.start()

    barrier = pltpu.get_barrier_semaphore()
    for name, peer in peers.items():
        @when(has[name])
        def _(peer=peer):
            pl.semaphore_signal(barrier, inc=1, device_id=peer, device_id_type=MESH)
    pl.semaphore_wait(barrier, 3 + jnp.where(has["up"], 1, 0) + jnp.where(has["down"], 1, 0))

    for copy in local[:3]:
        copy.wait()

    def block_copy(part, slot, name):
        start, rows = cuts[part]
        view = xc.at[slot, pl.ds(start, rows)]
        return pltpu.make_async_remote_copy(
            src_ref=view,
            dst_ref=view,
            send_sem=bs_sem.at[part, dirs[name], slot],
            recv_sem=br_sem.at[part, slot],
            device_id=peers[name],
            device_id_type=MESH,
        )

    block_copy(late, own, "y").start()
    for part in early:
        for name in ("up", "down", "y"):
            @when(has[name])
            def _(part=part, name=name):
                block_copy(part, own, name).start()
    for name in ("up", "down"):
        @when(has[name])
        def _(name=name):
            block_copy(late, own, name).start()

    chunks = wr_sem.shape[0]
    width = share // chunks

    def weight_copies(half, k, name, send_sem, recv_sem, mine):
        rows = pl.ds(pl.multiple_of((half * chunks + k) * width, width), width)
        pairs = (
            (wgu.at[rows, pl.ds(0, 2 * ff)], wgu.at[rows, pl.ds(2 * ff, 2 * ff)]),
            (wdn.at[rows, pl.ds(0, ff)], wdn.at[rows, pl.ds(ff, ff)]),
        )
        return [
            pltpu.make_async_remote_copy(
                src_ref=a if mine else b,
                dst_ref=b,
                send_sem=send_sem.at[k, n],
                recv_sem=recv_sem.at[k, n],
                device_id=peers[name],
                device_id_type=MESH,
            )
            for n, (a, b) in enumerate(pairs)
        ]

    def pair_weights(k):
        return weight_copies(sec, k, "x", xs_sem, xr_sem, True)

    def handed_weights(half, k):
        return weight_copies(half, k, "sec", ls_sem, lr_sem, False)

    for copy in local[3:]:
        copy.wait()
    for k in range(chunks):
        for copy in pair_weights(k):
            copy.start()

    block_copy(late, slot_of(1, z), "y").wait_recv()
    for name in ("up", "down"):
        @when(has[name])
        def _(name=name):
            block_copy(late, slot_of(1, z), name).start()

    lane = lax.broadcasted_iota(jnp.int32, (1, LANES), 1)
    pair = 2
    rows_step = pair * tok

    def inside(zz):
        return (zz >= 0) & (zz < z_count)

    def project(zz, q):
        slot = pair * zz
        expert = jnp.where(q == 0, me, partner)
        gu_cols = pl.ds(pl.multiple_of(q * 2 * ff, 2 * ff), 2 * ff)
        dn_cols = pl.ds(pl.multiple_of(q * ff, ff), ff)
        x = xc[pl.ds(slot, pair), :, pl.ds(0, depth)].reshape(rows_step, depth)
        c = xc[pl.ds(slot, pair), :, pl.ds(depth, depth)].reshape(rows_step, depth)
        w = xc[pl.ds(slot, pair), :, pl.ds(2 * depth, LANES)].reshape(rows_step, LANES)
        weight = jnp.sum(jnp.where(lane == expert, w.astype(f32), 0.0), axis=1, keepdims=True)
        gu = jnp.dot(x, wgu[:, gu_cols], preferred_element_type=f32)
        back = jnp.dot(c, wdn[:, dn_cols], preferred_element_type=f32)
        gate, up = gu[:, :ff], gu[:, ff:]
        sig = jax.nn.sigmoid(gate)
        silu = gate * sig
        hid = silu * up
        row_gate = jnp.sum(hid * back, axis=1, keepdims=True)
        d_hid = weight * back
        d_gate = (d_hid * up * sig * (1.0 + gate * (1.0 - sig))).astype(bf16)
        d_up = (d_hid * silu).astype(bf16)
        rows = pl.ds(pl.multiple_of(slot * tok, rows_step), rows_step)
        dgu[rows, gu_cols] = jnp.concatenate([d_gate, d_up], axis=1)
        whid[rows, dn_cols] = (weight * hid).astype(bf16)
        marked = jnp.where(lane == expert, row_gate, 0.0).astype(bf16).reshape(pair, tok, LANES)
        gates = (pl.ds(slot, pair), slice(None), pl.ds(depth, LANES))

        @pl.when(q == 0)
        def _():
            part_g[gates] = marked

        @pl.when(q == 1)
        def _():
            part_g[gates] = part_g[gates] + marked
            grads = lax.dot_general(
                dgu[rows, :], wgu[...], (((1,), (1,)), ((), ())), preferred_element_type=f32
            )
            part_g[pl.ds(slot, pair), :, pl.ds(0, depth)] = grads.astype(bf16).reshape(pair, tok, depth)

    swap_step = min(2, z_count)
    ways = ((-1, "up"), (1, "down"))

    def step(st, carry):
        @pl.when(st < z_count)
        def _():
            for part in early:
                for sign, onward in ways:
                    zz = z + sign * st

                    @pl.when(inside(zz))
                    def _(part=part, zz=zz, onward=onward):
                        block_copy(part, slot_of(0, zz), "y").wait_recv()

                        @when(has[onward])
                        def _():
                            block_copy(part, slot_of(0, zz), onward).start()

                        block_copy(part, slot_of(0, zz), "y").start()
            for sign, onward in ways:
                zz = z + sign * st

                @pl.when(inside(zz))
                def _(zz=zz, onward=onward):
                    for fp in (0, 1):
                        block_copy(late, slot_of(fp, zz), "y").wait_recv()

                        @when(has[onward])
                        def _(fp=fp):
                            block_copy(late, slot_of(fp, zz), onward).start()

        low = jnp.maximum(2 * st - 3, 0)
        count = 2 * st - 1 - low
        low_pair = jnp.where(st == swap_step, 0, low)
        count_pair = jnp.where(st < swap_step, 0, 2 * st - 1 - low_pair)

        def item(n, inner):
            q = jnp.where(n < count, 0, 1)
            place = jnp.where(n < count, low + n, low_pair + n - count)
            zz = z + ((place + 1) // 2) * (1 - 2 * (place % 2))

            @pl.when((n == count) & (st == swap_step))
            def _():
                for k in range(chunks):
                    for copy in pair_weights(k):
                        copy.wait_recv()
                    for copy in handed_weights(sec, k):
                        copy.start()
                for k in range(chunks):
                    for copy in handed_weights(1 - sec, k):
                        copy.wait_recv()

            @pl.when(inside(zz))
            def _():
                @pl.when(q == 0)
                def _():
                    for part in early:
                        block_copy(part, slot_of(1, zz), "y").wait_recv()

                project(zz, q)

            return inner

        lax.fori_loop(0, count + count_pair, item, 0)
        return carry

    lax.fori_loop(1, z_count + 1, step, 0)

    halves = ((0, split), (split, tok - split))

    def add_rows(slot, start, rows, view):
        def strip(k, carry):
            at = pl.ds(pl.multiple_of(start + k * ROW_TILE, ROW_TILE), ROW_TILE)
            off = pl.ds(pl.multiple_of(k * ROW_TILE, ROW_TILE), ROW_TILE)
            total = part_g[slot, at, :].astype(f32) + view[off, :].astype(f32)
            part_g[slot, at, :] = total.astype(bf16)
            return carry

        lax.fori_loop(0, rows // ROW_TILE, strip, 0)

    def p_copy(part, zz, slot):
        start, rows = halves[part]
        place = zz if part == 0 else z_count
        return pltpu.make_async_remote_copy(
            src_ref=part_g.at[slot, pl.ds(start, rows)],
            dst_ref=rp_a.at[zz] if part == 0 else rp_b,
            send_sem=ps_sem.at[place],
            recv_sem=pr_sem.at[place],
            device_id=peers["y"],
            device_id_type=MESH,
        )

    groups = ((0, 0, rz_a), (1, 0, rz_b.at[0]), (1, 1, rz_b.at[1]))

    def z_copy(group, dest, name, place):
        part, fp, buf = groups[group]
        start, rows = halves[part]
        return pltpu.make_async_remote_copy(
            src_ref=part_g.at[slot_of(fp, dest), pl.ds(start, rows)],
            dst_ref=buf.at[place],
            send_sem=zs_sem.at[group, dest],
            recv_sem=zr_sem.at[group, place],
            device_id=peers[name],
            device_id_type=MESH,
        )

    def z_take(group, dest, place):
        part, fp, buf = groups[group]
        start, rows = halves[part]
        z_copy(group, 0, "y", place).wait_recv()
        add_rows(slot_of(fp, dest), start, rows, buf.at[place])

    def z_send(group, dest):
        @pl.when(z < dest)
        def _():
            z_copy(group, dest, "up", dest).start()

        @pl.when(z > dest)
        def _():
            z_copy(group, dest, "down", jnp.where(z == dest + 1, z_count, dest)).start()

    def relays(dest):
        return ((z < dest) & (z > 0)) | ((z > dest) & (z < z_count - 1))

    def z_origin(group, dest):
        @pl.when(jnp.logical_not(relays(dest)))
        def _():
            z_send(group, dest)

    def z_relay(group, dest):
        @pl.when(relays(dest))
        def _():
            z_take(group, dest, dest)
            z_send(group, dest)

    def z_own(group):
        @pl.when(z > 0)
        def _():
            z_take(group, z, z)

        @pl.when(z < z_count - 1)
        def _():
            z_take(group, z, z_count)

    def chunk_rows(k):
        return pl.ds(pl.multiple_of(k * width, width), width)

    def out_copy(k):
        at = chunk_rows(k)
        return pltpu.make_async_copy(wacc.at[:, at, :], grad_out.at[:, at, :], out_sem.at[k])

    def chunk_copy(k, src, dst, send_sem, recv_sem, name):
        return pltpu.make_async_remote_copy(
            src_ref=src.at[chunk_rows(k)],
            dst_ref=dst.at[chunk_rows(k)],
            send_sem=send_sem.at[k],
            recv_sem=recv_sem.at[k],
            device_id=peers[name],
            device_id_type=MESH,
        )

    def sib_copy(k):
        return chunk_copy(k, sib_send, sib_recv, ss_sem, sr_sem, "sec")

    def pair_copy(k):
        return chunk_copy(k, pair_send, pair_recv, ws_sem, wr_sem, "x")

    fold = (((0,), (0,)), ((), ()))

    for zz in order_z:
        p_copy(0, zz, slot_of(1, zz)).start()
        z_origin(2, zz)
        z_origin(1, zz)

    def returned(i, carry):
        @pl.when(i < 2 * chunks)
        def _():
            k = i // 2
            away = i % 2 == 0
            half = jnp.where(away, 1 - sec, sec)
            col = (half * chunks + k) * width
            xs = xc[:, :, pl.ds(pl.multiple_of(col, width), width)].reshape(-1, width)
            cs = xc[:, :, pl.ds(pl.multiple_of(depth + col, width), width)].reshape(-1, width)
            got_gu = lax.dot_general(xs, dgu[...], fold, preferred_element_type=f32)
            got_dn = lax.dot_general(cs, whid[...], fold, preferred_element_type=f32)

            @pl.when(away)
            def _():
                sib_send[chunk_rows(k), pl.ds(0, 4 * ff)] = got_gu.astype(bf16)
                sib_send[chunk_rows(k), pl.ds(4 * ff, 2 * ff)] = got_dn.astype(bf16)
                sib_copy(k).start()

            @pl.when(jnp.logical_not(away))
            def _():
                sib_copy(k).wait_recv()
                all_gu = got_gu + sib_recv[chunk_rows(k), pl.ds(0, 4 * ff)].astype(f32)
                all_dn = got_dn + sib_recv[chunk_rows(k), pl.ds(4 * ff, 2 * ff)].astype(f32)
                pair_send[chunk_rows(k), pl.ds(0, 2 * ff)] = all_gu[:, 2 * ff:].astype(bf16)
                pair_send[chunk_rows(k), pl.ds(2 * ff, ff)] = all_dn[:, ff:].astype(bf16)
                pair_copy(k).start()
                wacc[0, chunk_rows(k), :] = all_gu[:, :ff]
                wacc[1, chunk_rows(k), :] = all_gu[:, ff : 2 * ff]
                wacc[2, chunk_rows(k), :] = all_dn[:, :ff]

        turn = (i - 3) // 2

        @pl.when((i >= 3) & (i % 2 == 1))
        def _():
            dest = pick(order_z, turn)

            @pl.when(turn == 0)
            def _():
                for zz in order_z:
                    z_relay(2, zz)
                    z_relay(1, zz)

            p_copy(0, dest, own).wait_recv()
            add_rows(slot_of(0, dest), 0, split, rp_a.at[dest])
            z_origin(0, dest)

            @pl.when(turn >= 1)
            def _():
                z_relay(0, pick(order_z, (turn + z_count - 1) % z_count))

            @pl.when(turn == z_count - 2)
            def _():
                z_own(2)
                p_copy(1, z, slot_of(1, z)).start()

        return carry

    lax.fori_loop(0, max(2 * chunks, 2 * z_count + 2), returned, 0)

    z_relay(0, order_z[-1])
    p_copy(1, z, own).wait_recv()
    add_rows(own, split, tok - split, rp_b)
    z_own(1)
    z_own(0)
    token_copies = (
        pltpu.make_async_copy(part_g.at[own, :, pl.ds(0, depth)], tok_out, loc_sem.at[0]),
        pltpu.make_async_copy(part_g.at[own, :, pl.ds(depth, LANES)], gate_out, loc_sem.at[1]),
    )
    for copy in token_copies:
        copy.start()

    def finish(k, carry):
        pair_copy(k).wait_recv()
        for m in range(3):
            other = pair_recv[chunk_rows(k), pl.ds(m * ff, ff)].astype(f32)
            wacc[m, chunk_rows(k), :] = (wacc[m, chunk_rows(k), :] + other) / sections
        out_copy(k).start()
        return carry

    lax.fori_loop(0, chunks, finish, 0)

    for copy in token_copies:
        copy.wait()
    for k in range(chunks):
        out_copy(k).wait()
        sib_copy(k).wait_send()
        pair_copy(k).wait_send()
        for copy in pair_weights(k):
            copy.wait_send()
        for copy in handed_weights(sec, k):
            copy.wait_send()
    block_copy(late, own, "y").wait_send()
    for name in ("up", "down"):
        @when(has[name])
        def _(name=name):
            for part in (*early, late):
                block_copy(part, own, name).wait_send()
            block_copy(late, slot_of(1, z), name).wait_send()
    for part in early:
        block_copy(part, own, "y").wait_send()

    def drain(st, carry):
        for sign, onward in ways:
            zz = z + sign * st

            @pl.when(inside(zz))
            def _(zz=zz, onward=onward):
                for part in early:
                    block_copy(part, slot_of(0, zz), "y").wait_send()

                @when(has[onward])
                def _():
                    for part in early:
                        block_copy(part, slot_of(0, zz), onward).wait_send()
                    for fp in (0, 1):
                        block_copy(late, slot_of(fp, zz), onward).wait_send()

        return carry

    lax.fori_loop(1, z_count, drain, 0)
    for zz in range(z_count):
        p_copy(0, zz, own).wait_send()
    p_copy(1, z, own).wait_send()
    for group in range(3):
        for dest in range(z_count):
            @pl.when(z != dest)
            def _():
                z_copy(group, dest, "y", dest).wait_send()


def gathered(tokens, cotangent, routes, route_weights, weights):
    experts = lax.axis_size("expert")
    sections = lax.axis_size("section")
    z_count = experts // 4
    blocks = 2 * z_count
    tok, depth = tokens.shape[1:]
    ff = weights.shape[3]
    named = routes[0][:, :, None] == jnp.arange(LANES, dtype=jnp.int32)
    dense_w = jnp.sum(jnp.where(named, route_weights[0][:, :, None], 0), axis=1)
    unit = tok // 8 // ROW_TILE * ROW_TILE
    split = 7 * unit
    cuts = ((0, 4 * unit), (4 * unit, 3 * unit), (split, tok - split))
    bf16 = jnp.bfloat16
    g_width = depth + LANES
    share = depth // sections
    chunks = max(1, share // 256)
    dma = pltpu.SemaphoreType.DMA
    any_spec = pl.BlockSpec(memory_space=pl.ANY)
    token_grads, gates, grads = pl.pallas_call(
        functools.partial(fused_kernel, experts, split, cuts),
        out_shape=(
            jax.ShapeDtypeStruct((tok, depth), bf16),
            jax.ShapeDtypeStruct((tok, LANES), bf16),
            jax.ShapeDtypeStruct((3, share, ff), jnp.float32),
        ),
        in_specs=[any_spec] * 4,
        out_specs=(any_spec,) * 3,
        scratch_shapes=[
            pltpu.VMEM((blocks, tok, 2 * depth + LANES), bf16),
            pltpu.VMEM((blocks, tok, g_width), bf16),
            pltpu.VMEM((depth, 4 * ff), bf16),
            pltpu.VMEM((depth, 2 * ff), bf16),
            pltpu.VMEM((blocks * tok, 4 * ff), bf16),
            pltpu.VMEM((blocks * tok, 2 * ff), bf16),
            pltpu.VMEM((share, 6 * ff), bf16),
            pltpu.VMEM((share, 6 * ff), bf16),
            pltpu.VMEM((share, 3 * ff), bf16),
            pltpu.VMEM((share, 3 * ff), bf16),
            pltpu.VMEM((3, share, ff), jnp.float32),
            pltpu.VMEM((z_count + 1, split, g_width), bf16),
            pltpu.VMEM((2, z_count + 1, tok - split, g_width), bf16),
            pltpu.VMEM((z_count, split, g_width), bf16),
            pltpu.VMEM((tok - split, g_width), bf16),
            dma((6,)),
            dma((len(cuts), 3, blocks)),
            dma((len(cuts), blocks)),
            dma((chunks, 2)),
            dma((chunks, 2)),
            dma((chunks, 2)),
            dma((chunks, 2)),
            dma((3, z_count)),
            dma((3, z_count + 1)),
            dma((z_count + 1,)),
            dma((z_count + 1,)),
            dma((chunks,)),
            dma((chunks,)),
            dma((chunks,)),
            dma((chunks,)),
            dma((chunks,)),
        ],
        compiler_params=pltpu.CompilerParams(
            collective_id=0, has_side_effects=True, vmem_limit_bytes=67043328
        ),
    )(tokens[0], cotangent[0], dense_w, weights[:, 0])
    gate_grads = jnp.sum(jnp.where(named, gates[:, None, :], 0), axis=2)[None]
    return (token_grads[None], gate_grads, grads[:, None])


def exchanged(tokens, cotangent, routes, route_weights, weights):
    experts = lax.axis_size("expert")
    tok_count, depth = tokens.shape[1:]
    top_k = routes.shape[-1]
    capacity = min(tok_count, max(2, (9 * tok_count * top_k + 8 * experts - 1) // (8 * experts)))
    route_block = routes[0]
    slots, slot_table = slot_assign(route_block, experts, capacity)
    token_ix = slot_table // top_k
    zero_row = jnp.zeros((1, depth), tokens.dtype)
    send_in = jnp.concatenate([tokens[0], zero_row])[token_ix]
    send_cot = jnp.concatenate([cotangent[0], zero_row])[token_ix]
    send_weight = jnp.concatenate(
        [route_weights[0].reshape(-1), jnp.zeros((1,), route_weights.dtype)]
    )[slot_table]
    recv_in, recv_cot, recv_weight = (
        lax.all_to_all(block, "expert", split_axis=0, concat_axis=0, tiled=True)
        for block in (send_in, send_cot, send_weight)
    )
    row_gate, row_grads, weight_part = expert_math(
        recv_in.reshape(-1, depth), recv_cot.reshape(-1, depth), recv_weight.reshape(-1), weights[:, 0]
    )
    back_rows, back_gate = (
        lax.all_to_all(block, "expert", split_axis=0, concat_axis=0, tiled=True)
        for block in (
            row_grads.reshape(experts, capacity, depth),
            row_gate.reshape(experts, capacity),
        )
    )
    flat_rows = back_rows.reshape(experts * capacity, depth)
    flat_index = route_block * capacity + slots
    accum = jnp.zeros((tok_count, depth), jnp.float32)
    for position in range(top_k):
        accum = accum + flat_rows[flat_index[:, position]].astype(jnp.float32)
    token_grads = accum.astype(jnp.bfloat16)[None]
    gate_grads = back_gate.reshape(-1)[flat_index][None]
    return (token_grads, gate_grads, section_mean(weight_part))


def solution(mesh):
    placed = P("section", "expert", None)

    def per_device(tokens, cotangent, routes, route_weights, weights):
        dense = 4 * routes.shape[-1] >= lax.axis_size("expert")
        plan = gathered if dense else exchanged
        return plan(tokens, cotangent, routes, route_weights, weights)

    return jax.shard_map(
        per_device,
        mesh=mesh,
        in_specs=(placed, placed, placed, placed, P(None, "expert", None, None)),
        out_specs=(placed, placed, P(None, "expert", "section", None)),
        check_vma=False,
    )
```
